128 devices in a mesh: energy: 16 (over y, z_hi, core), section: 8 (over z_lo, x).
Axes of the slice: x: 4, y: 4, z: 4 (z_hi: 2, z_lo: 2; z = z_hi * 2 + z_lo), core: 2. Of those that a mesh axis runs over, the one named last changes fastest.
Arguments:
- self_in: float32 [64, 8, 2, 256, 256], P('energy', 'section'), as said below
- onsite: float32 [8, 256], P('section'), may hold values from -1 to 1
- within: float32 [8, 256, 256], P('section'), may hold values from -0.09375 to 0.09375
- between: float32 [8, 256, 256], P('section'), as said below
- coupling: float32 [8, 256, 256], P('section'), may hold values from -1 to 1
- groups: int32 [8, 256], P('section'), may hold values from 0 to 3
- offsets: int32 [3], replicated, may hold values from 1 to 2, as said below
- strength: float32 [3], replicated, may hold values from 0.3 to 1
Outputs:
- green: float32 [64, 8, 2, 256, 256], P('energy', 'section')
- self_out: float32 [64, 8, 2, 256, 256], P('energy', 'section')
The draws below stay inside these ranges and needn't reach their ends.
Inputs may be any that keep to these rules, and one draw needn't show every extreme that they name: `offsets`: every entry lies between 1 and 2, and one entry equals 2. `self_in`: imaginary parts of diagonal entries lie between -0.02 and -0.002, real parts of diagonal entries between -0.3 and 0.3; off-diagonal entries lie between -0.01 and 0.01. `between`: diagonal entries lie between 1.4 and 2.0; off-diagonal entries are at most 1.12 / sqrt(256) in magnitude.
All inputs are finite; a program needn't handle non-finite values.
Results may differ from the reference program's by a relative error of at most 0.0001.
Values sent between devices are 32-bit elements; how exact they have to be, the bound alone decides.
No kernel may reach another device: no remote copies, remote signals or barrier semaphores. Data moves between devices by JAX's collectives and lax.ppermute only.
A program may use at most 128 MiB of HBM per device.

```python
import math
import jax
import jax.numpy as jnp
from jax import lax

B = 256
NEWTON = 3
MODES = 3
GROUPS = 4
OFF_MAX = 2
ENERGIES = 64
SLABS = 8


def draw_self_in(key, part):
    shape = (ENERGIES, SLABS, 2, B, B)
    first_key = jax.random.fold_in(key, 11)
    second_key = jax.random.fold_in(key, 12)
    third_key = jax.random.fold_in(key, 13)
    spread = jnp.clip(0.004 * jax.random.normal(first_key, shape, jnp.float32), -0.01, 0.01)
    real_diag = jax.random.uniform(second_key, (ENERGIES, SLABS, B), jnp.float32, -0.3, 0.3)
    imag_diag = jax.random.uniform(third_key, (ENERGIES, SLABS, B), jnp.float32, -0.02, -0.002)
    identity = jnp.eye(B, dtype=jnp.float32)
    diagonal = jnp.stack([real_diag, imag_diag], axis=2)[..., :, None] * identity
    return spread * (1.0 - identity) + diagonal


def draw_between(key, part):
    diag_key = jax.random.fold_in(key, 31)
    rest_key = jax.random.fold_in(key, 32)
    identity = jnp.eye(B, dtype=jnp.float32)
    diag_values = jax.random.uniform(diag_key, (SLABS, B), jnp.float32, 1.4, 2.0)
    scale = 0.28 * B ** (-0.5)
    rest = jnp.clip(scale * jax.random.normal(rest_key, (SLABS, B, B), jnp.float32), -4.0 * scale, 4.0 * scale)
    return rest * (1.0 - identity) + diag_values[:, :, None] * identity


def draw_offsets(key, part):
    values = jax.random.randint(jax.random.fold_in(key, 21), (MODES,), 1, OFF_MAX + 1)
    chosen = jax.random.randint(jax.random.fold_in(key, 22), (), 0, MODES)
    return jnp.where(jnp.arange(MODES) == chosen, OFF_MAX, values).astype(jnp.int32)


def touch_ends(values, stream_key, low, largest):
    extent = values.shape
    index_at = [jax.random.randint(jax.random.fold_in(stream_key, axis), (), 0, extent[axis]) for axis in range(len(extent))]
    values = values.at[tuple(index_at)].set(low)
    longest = extent.index(max(extent))
    index_at[longest] = (index_at[longest] + 1) % extent[longest]
    return values.at[tuple(index_at)].set(largest)


def shard_levels(key, shape, cuts, low, largest):
    loudness, own = 1.0, jax.random.fold_in(key, 6)
    for axis_at, parts in cuts:
        steps = jnp.exp(jax.random.uniform(jax.random.fold_in(own, axis_at), (parts,), jnp.float32, low / len(cuts), largest / len(cuts)))
        loudness = loudness * jnp.repeat(steps, shape[axis_at] // parts).reshape([-1 if axis == axis_at else 1 for axis in range(len(shape))])
    return loudness


def normal_values(key, shape, scale, reach, shards=(), kind=jnp.bfloat16):
    level = shard_levels(key, shape, shards, -0.22, 0.18) if shards else 1.0
    array = jax.random.normal(key, shape, jnp.float32) * scale * level
    return jnp.minimum(jnp.maximum(array, -reach), reach).astype(kind)


def setup_inputs(seed: int = 0) -> dict:
    arg_keys = jax.random.split(jax.random.key(seed), 9)
    self_in = draw_self_in(jax.random.fold_in(arg_keys[8], 71), 0)
    onsite = jnp.clip(jax.random.uniform(arg_keys[1], (SLABS, B), jnp.float32, -1.0, 1.0) * shard_levels(arg_keys[1], (SLABS, B), ((0, 8),), -0.4, 0.0), -1.0, 1.0)
    within = normal_values(arg_keys[2], (SLABS, B, B), (16 * B) ** -0.5, 0.09375, ((0, 8),), jnp.float32)
    between = draw_between(jax.random.fold_in(arg_keys[8], 71), 0)
    coupling = normal_values(arg_keys[4], (SLABS, B, B), 0.18, 1.0, ((0, 8),), jnp.float32)
    groups = touch_ends(jax.random.randint(arg_keys[5], (SLABS, B), 0, GROUPS), jax.random.fold_in(arg_keys[5], 1), 0, GROUPS - 1).astype(jnp.int32)
    offsets = draw_offsets(jax.random.fold_in(arg_keys[8], 71), 0)
    strength = jnp.clip(jnp.exp(jax.random.uniform(arg_keys[7], (MODES,), jnp.float32, math.log(0.3), math.log(1.0))), 0.3, 1.0)
    return {"self_in": self_in, "onsite": onsite, "within": within, "between": between, "coupling": coupling, "groups": groups, "offsets": offsets, "strength": strength}


HIGH = lax.Precision.HIGHEST
ETA = 1.0
CONTACT = 0.6


def multiply(left, right):
    return jnp.einsum("...ij,...jk->...ik", left, right, precision=HIGH)


def product(left, right):
    real_a, imag_a = left[..., 0, :, :], left[..., 1, :, :]
    real_b, imag_b = right[..., 0, :, :], right[..., 1, :, :]
    return jnp.stack([multiply(real_a, real_b) - multiply(imag_a, imag_b),
                      multiply(real_a, imag_b) + multiply(imag_a, real_b)], axis=-3)


def times_real(field, matrix):
    return jnp.einsum("...ij,jk->...ik", field, matrix, precision=HIGH)


def real_times(matrix, field):
    return jnp.einsum("ij,...jk->...ik", matrix, field, precision=HIGH)


def newton(system):
    sys_re, sys_im = system[..., 0, :, :], system[..., 1, :, :]
    real_c = jnp.diagonal(sys_re, axis1=-2, axis2=-1)
    imag_c = jnp.diagonal(sys_im, axis1=-2, axis2=-1)
    modulus = real_c * real_c + imag_c * imag_c
    inv_re = real_c / modulus
    inv_im = -imag_c / modulus
    half_re = inv_re[..., :, None] * sys_re - inv_im[..., :, None] * sys_im
    half_im = inv_re[..., :, None] * sys_im + inv_im[..., :, None] * sys_re
    full_re = half_re * inv_re[..., None, :] - half_im * inv_im[..., None, :]
    full_im = half_re * inv_im[..., None, :] + half_im * inv_re[..., None, :]
    identity = jnp.eye(system.shape[-1], dtype=jnp.float32)
    iterate = jnp.stack([2.0 * inv_re[..., :, None] * identity - full_re,
                         2.0 * inv_im[..., :, None] * identity - full_im], axis=-3)
    for sweep in range(NEWTON - 1):
        iterate = 2.0 * iterate - product(iterate, product(system, iterate))
    return iterate


def local_inverse(energy, hamil, sigma, previous, hop):
    identity = jnp.eye(hamil.shape[-1], dtype=jnp.float32)
    left = real_times(hop.T, times_real(previous, hop))
    sys_re = energy[..., None, None] * identity - hamil - sigma[..., 0, :, :] - left[..., 0, :, :]
    sys_im = ETA * identity - sigma[..., 1, :, :] - left[..., 1, :, :]
    return newton(jnp.stack([sys_re, sys_im], axis=-3))


def refine(local_green, incoming):
    return local_green + product(local_green, product(incoming, local_green))


def sandwich(hop, green):
    return times_real(real_times(hop, green), hop.T)


def reference(self_in, onsite, within, between, coupling, groups, offsets, strength):
    width = onsite.shape[1]
    identity = jnp.eye(width, dtype=jnp.float32)
    hams = onsite[:, :, None] * identity + 0.5 * (within + jnp.swapaxes(within, 1, 2))
    energies = -1.0 + (2 * jnp.arange(ENERGIES, dtype=jnp.int32) + 1).astype(jnp.float32) / ENERGIES
    contact = jnp.stack([jnp.zeros((width, width), jnp.float32), -CONTACT * identity])

    def one_energy(inputs):
        energy, sigma_all = inputs

        def forward(previous, items):
            hamil, hop, sigma = items
            local_green = local_inverse(energy, hamil, sigma, previous, hop)
            return local_green, local_green

        _, locals_all = lax.scan(forward, contact, (hams, between, sigma_all))

        def backward(incoming, items):
            local_green, hop = items
            full = refine(local_green, incoming)
            return sandwich(hop, full), full

        _, greens = lax.scan(backward, jnp.zeros((2, width, width), jnp.float32),
                             (locals_all, between), reverse=True)
        return greens

    green = lax.map(one_energy, (energies, self_in))
    padded = jnp.pad(green, ((OFF_MAX, OFF_MAX), (0, 0), (0, 0), (0, 0), (0, 0)))
    summed = jnp.zeros_like(green)
    for mode in range(MODES):
        shift = offsets[mode].astype(jnp.int32)
        lower = lax.dynamic_slice_in_dim(padded, (OFF_MAX - shift).astype(jnp.int32), ENERGIES, 0)
        upper = lax.dynamic_slice_in_dim(padded, (OFF_MAX + shift).astype(jnp.int32), ENERGIES, 0)
        summed = summed + strength[mode] * (lower + upper)
    mats = jnp.where(groups[:, :, None] == groups[:, None, :], coupling, jnp.float32(0.0))
    first = jnp.einsum("sab,eszbc->eszac", mats, summed, precision=HIGH)
    self_out = jnp.einsum("eszac,sdc->eszad", first, mats, precision=HIGH)
    return green, self_out
```

```python
import functools

import jax
import jax.numpy as jnp
from jax import lax
from jax.experimental import pallas as pl
from jax.experimental.pallas import tpu as pltpu
from jax.sharding import PartitionSpec as P

MODES = 3
ETA = 1.0
CONTACT = 0.6
ENERGIES = 64
W = 256
X = 4
AXES = ("energy", "section")
F32 = jnp.float32
BF16 = jnp.bfloat16


def split(value):
    high = value.astype(BF16)
    return high, (value - high.astype(F32)).astype(BF16)


def dot(left, right):
    return lax.dot_general(left, right, (((1,), (0,)), ((), ())), preferred_element_type=F32)


def dot3(left, right):
    return dot(left[0], right[0]) + (dot(left[0], right[1]) + dot(left[1], right[0]))


def complex_split(real, imag):
    return split(real), split(imag), split(real + imag)


def complex_product(left, right):
    first = dot3(left[0], right[0])
    second = dot3(left[1], right[1])
    third = dot3(left[2], right[2])
    return first - second, third - (first + second)


def on_diagonal():
    rows = lax.broadcasted_iota(jnp.int32, (W, W), 0)
    return rows == lax.broadcasted_iota(jnp.int32, (W, W), 1)


def forward_slab(sys_re, sys_im, hop, hop_t, prev_re, prev_im):
    sys_re = sys_re - dot3(hop_t, split(dot3(split(prev_re), hop)))
    sys_im = sys_im - dot3(hop_t, split(dot3(split(prev_im), hop)))
    diagonal = on_diagonal()

    def inverse_diagonal(axis):
        real = jnp.sum(jnp.where(diagonal, sys_re, 0.0), axis=axis, keepdims=True)
        imag = jnp.sum(jnp.where(diagonal, sys_im, 0.0), axis=axis, keepdims=True)
        modulus = real * real + imag * imag
        return real / modulus, -imag / modulus

    col_re, col_im = inverse_diagonal(1)
    row_re, row_im = inverse_diagonal(0)
    r1_re = jnp.where(diagonal, 0.0, col_im * sys_im - col_re * sys_re)
    r1_im = jnp.where(diagonal, 0.0, -(col_re * sys_im + col_im * sys_re))
    r1 = complex_split(r1_re, r1_im)
    r2_re, r2_im = complex_product(r1, r1)
    r2 = complex_split(r2_re, r2_im)
    r3_re, r3_im = complex_product(r2, r1)
    r4_re, r4_im = complex_product(r2, r2)
    sum_re = jnp.where(diagonal, 1.0, 0.0) + r1_re + r2_re + r3_re
    sum_im = r1_im + r2_im + r3_im
    out_re, out_im = complex_product(complex_split(r4_re, r4_im), complex_split(sum_re, sum_im))
    out_re, out_im = out_re + sum_re, out_im + sum_im
    return out_re * row_re - out_im * row_im, out_re * row_im + out_im * row_re


def backward_slab(loc_re, loc_im, hop, hop_t, in_re, in_im):
    local = complex_split(loc_re, loc_im)
    half = complex_split(*complex_product(local, complex_split(in_re, in_im)))
    add_re, add_im = complex_product(half, local)
    full_re, full_im = loc_re + add_re, loc_im + add_im
    sent_re = dot3(split(dot3(hop, split(full_re))), hop_t)
    sent_im = dot3(split(dot3(hop, split(full_im))), hop_t)
    return full_re, full_im, sent_re, sent_im


def place():
    section = lax.axis_index("section")
    return section % X, section // X, lax.axis_index("energy") % 2


def system_kernel(self_ref, onsite_ref, within_ref, first_ref, *outs):
    x, _, _ = place()
    diagonal = on_diagonal()
    within = within_ref[0]
    base = 0.5 * (within + within.T)
    base = base + jnp.where(diagonal, onsite_ref[...], 0.0)
    for turn in range(X):
        index = lax.rem(x + turn, X)
        number = first_ref[0] + index
        energy = -1.0 + (2 * number + 1).astype(F32) / ENERGIES
        outs[turn][0] = jnp.where(diagonal, energy, 0.0) - base - self_ref[index, 0, 0]
        outs[turn][1] = jnp.where(diagonal, ETA, 0.0) - self_ref[index, 0, 1]


def load_hops(hop_refs, hops, sems):
    x, _, core = place()
    own, direct, swapped, half, other = hop_refs
    before, after = lax.rem(x + X - 1, X), lax.rem(x + 1, X)
    far = lax.rem(x + 2, X)
    rows = W // 2
    return [
        pltpu.make_async_copy(own.at[0], hops.at[x], sems.at[0]),
        pltpu.make_async_copy(direct, hops.at[jnp.where(core == 0, before, after)], sems.at[1]),
        pltpu.make_async_copy(swapped, hops.at[jnp.where(core == 0, after, before)], sems.at[2]),
        pltpu.make_async_copy(half, hops.at[far, pl.ds(core * rows, rows)], sems.at[3]),
        pltpu.make_async_copy(other, hops.at[far, pl.ds((1 - core) * rows, rows)], sems.at[4]),
    ]


def split_hops(hops, parts):
    high, low, high_t, low_t = parts
    for slab in range(X):
        high[slab], low[slab] = split(hops[slab])
        high_t[slab], low_t[slab] = split(hops[slab].T)


def hop_of(parts, slab):
    high, low, high_t, low_t = parts
    return (high[slab], low[slab]), (high_t[slab], low_t[slab])


def recursion_kernel(mode, *refs):
    x, z, _ = place()
    ins, refs = refs[:4], refs[4:]
    hop_refs, refs = refs[:5], refs[5:]
    message_in, refs = refs[0], refs[1:]
    if mode == "last":
        outs, refs = refs[:4], refs[4:]
        message_out = None
    elif mode == "middle":
        outs, message_out, refs = refs[:4], refs[4], refs[5:]
    else:
        outs, message_out, refs = refs[:1], refs[1], refs[2:]
    blocks, carried, hops, *parts, in_sems, hop_sems, out_sems, carry_sem = refs

    @pl.when(z == (1 if mode == "middle" else 0))
    def _():
        copies = load_hops(hop_refs, hops, hop_sems)
        if mode == "last":
            copies += [pltpu.make_async_copy(ins[0], blocks, in_sems.at[0])]
        else:
            copies += [
                pltpu.make_async_copy(
                    ins[turn], blocks.at[lax.rem(x - turn + X, X)], in_sems.at[turn]
                )
                for turn in range(X)
            ]
        if mode != "first":
            copies.append(pltpu.make_async_copy(message_in, carried, carry_sem))
        for copy in copies:
            copy.start()
        for copy in copies:
            copy.wait()
        split_hops(hops, parts)
        if mode == "first":
            carried[0] = jnp.zeros((W, W), F32)
            carried[1] = jnp.where(on_diagonal(), -CONTACT, 0.0)

        if mode != "last":

            def advance(slab, unused):
                hop, hop_t = hop_of(parts, slab)
                real, imag = forward_slab(
                    blocks[slab, 0], blocks[slab, 1], hop, hop_t, carried[0], carried[1]
                )
                blocks[slab, 0], blocks[slab, 1] = real, imag
                carried[0], carried[1] = real, imag
                return unused

            lax.fori_loop(0, X, advance, 0)

        if mode == "middle":
            carried[...] = jnp.zeros_like(carried)

        if mode != "first":

            def retreat(step, unused):
                slab = X - 1 - step
                hop, hop_t = hop_of(parts, slab)
                real, imag, sent_re, sent_im = backward_slab(
                    blocks[slab, 0], blocks[slab, 1], hop, hop_t, carried[0], carried[1]
                )
                blocks[slab, 0], blocks[slab, 1] = real, imag
                carried[0], carried[1] = sent_re, sent_im
                return unused

            lax.fori_loop(0, X, retreat, 0)
            copies = [
                pltpu.make_async_copy(
                    blocks.at[lax.rem(x + turn, X)], outs[turn], out_sems.at[turn]
                )
                for turn in range(X)
            ]
        else:
            copies = [pltpu.make_async_copy(blocks, outs[0], out_sems.at[0])]
        if message_out is not None:
            copies.append(pltpu.make_async_copy(carried, message_out, carry_sem))
        for copy in copies:
            copy.start()
        for copy in copies:
            copy.wait()


ANY = pl.BlockSpec(memory_space=pl.ANY)
VMEM = pl.BlockSpec(memory_space=pltpu.VMEM)
SMEM = pl.BlockSpec(memory_space=pltpu.SMEM)
BLOCK = jax.ShapeDtypeStruct((2, W, W), F32)
SLABS4 = jax.ShapeDtypeStruct((X, 2, W, W), F32)


def cost(products):
    return pl.CostEstimate(flops=products * 6 * W**3, bytes_accessed=6 << 20, transcendentals=0)


def recursion(mode, ins, hop_refs, message_in):
    if mode == "first":
        out_shape = (SLABS4, BLOCK)
    elif mode == "middle":
        out_shape = (BLOCK,) * 5
    else:
        out_shape = (BLOCK,) * 4
    return pl.pallas_call(
        functools.partial(recursion_kernel, mode),
        out_shape=out_shape,
        in_specs=[ANY] * 10,
        out_specs=[ANY] * len(out_shape),
        scratch_shapes=[
            pltpu.VMEM((X, 2, W, W), F32),
            pltpu.VMEM((2, W, W), F32),
            pltpu.VMEM((X, W, W), F32),
        ]
        + [pltpu.VMEM((X, W, W), BF16)] * 4
        + [
            pltpu.SemaphoreType.DMA((4,)),
            pltpu.SemaphoreType.DMA((5,)),
            pltpu.SemaphoreType.DMA((4,)),
            pltpu.SemaphoreType.DMA,
        ],
        name=f"recursion_{mode}",
        cost_estimate=cost({"first": 64, "middle": 104, "last": 40}[mode]),
    )(*ins, *hop_refs, message_in)


def scatter_kernel(*refs):
    strength_ref, offsets_ref, coupling_ref, groups_ref, groups_t_ref = refs[:5]
    early, late = refs[5:9], refs[9:13]
    halo_early, halo_late = refs[13:17], refs[17:21]
    green_ref, self_ref = refs[21:23]
    own, side, out, in_sems, out_sems = refs[23:]
    x, z, _ = place()

    def fetch(sets):
        copies = []
        for turn in range(X):
            index = lax.rem(x - turn + X, X)
            copies.append(
                pltpu.make_async_copy(sets[0][turn], own.at[index], in_sems.at[turn])
            )
            copies.append(
                pltpu.make_async_copy(sets[1][turn], side.at[index], in_sems.at[X + turn])
            )
        return copies

    @pl.when(z == 1)
    def _():
        for copy in fetch((early, halo_early)):
            copy.start()

    @pl.when(z == 0)
    def _():
        for copy in fetch((late, halo_late)):
            copy.start()

    weights = []
    for distance in (1, 2):
        weights.append(
            sum(
                jnp.where(offsets_ref[mode] == distance, strength_ref[mode], 0.0)
                for mode in range(MODES)
            )
        )
    matrix = jnp.where(groups_ref[...] == groups_t_ref[...], coupling_ref[0], 0.0)
    left, right = split(matrix), split(matrix.T)
    for copy in fetch((late, halo_late)):
        copy.wait()
    store = [
        pltpu.make_async_copy(own.at[i], green_ref.at[i, 0], out_sems.at[i]) for i in range(X)
    ]
    for copy in store:
        copy.start()

    def energy(index):
        return side[index + X] if index < 0 else own[index] if index < X else side[index - X]

    for index in range(X):
        near = energy(index - 1) + energy(index + 1)
        far = energy(index - 2) + energy(index + 2)
        total = weights[0] * near + weights[1] * far
        for part in range(2):
            out[index, part] = dot3(split(dot3(left, split(total[part]))), right)
        copy = pltpu.make_async_copy(out.at[index], self_ref.at[index, 0], out_sems.at[X + index])
        copy.start()
        store.append(copy)
    for copy in store:
        copy.wait()


def send(value, pairs):
    return lax.ppermute(value, AXES, pairs)


def per_device(self_in, onsite, within, between, coupling, groups, offsets, strength):
    count, sections = lax.axis_size("energy"), lax.axis_size("section")
    x, _, core = place()
    chunks, lanes = range(count), range(sections)

    def device(chunk, section):
        return chunk * sections + section

    def shifted(section, turn):
        return section // X * X + (section + turn) % X

    half = lax.dynamic_slice_in_dim(between[0], core * (W // 2), W // 2, 0)
    direct = send(
        between[0],
        [(device(c, s), device(c, shifted(s, 1 if c % 2 == 0 else -1))) for c in chunks for s in lanes],
    )
    far = send(half, [(device(c, s), device(c, shifted(s, 2))) for c in chunks for s in lanes])
    partner = [(device(c, s), device(c ^ 1, s)) for c in chunks for s in lanes]
    hop_refs = (between, direct, send(direct, partner), far, send(far, partner))

    first_index = (lax.axis_index("energy") * X).reshape(1)
    systems = pl.pallas_call(
        system_kernel,
        out_shape=(BLOCK,) * X,
        in_specs=[VMEM, VMEM, VMEM, SMEM],
        out_specs=[VMEM] * X,
        name="systems",
    )(self_in, onsite, within, first_index)

    def exchange(values, halves):
        return (values[0],) + tuple(
            send(
                values[turn],
                [(device(c, s), device(c, shifted(s, turn))) for c in chunks for s in lanes if s // X in halves],
            )
            for turn in range(1, X)
        )

    def halo(values, half):
        result = []
        for turn in range(X):
            pairs = []
            for c in chunks:
                for s in lanes:
                    target = c - 1 if (s - turn) % X < 2 else c + 1
                    if s // X == half and 0 <= target < count:
                        pairs.append((device(c, s), device(target, s)))
            result.append(send(values[turn], pairs))
        return tuple(result)

    blocks = exchange(systems, (0, 1))
    up = [(device(c, s), device(c, s + X)) for c in chunks for s in range(X)]
    down = [(target, source) for source, target in up]
    locals_low, message = recursion("first", blocks, hop_refs, blocks[0])
    message = send(message, up)
    *greens_high, message = recursion("middle", blocks, hop_refs, message)
    message = send(message, down)
    early = exchange(greens_high, (1,))
    halo_early = halo(early, 1)
    greens_low = recursion("last", (locals_low,) * 4, hop_refs, message)
    late = exchange(greens_low, (0,))
    halo_late = halo(late, 0)

    return pl.pallas_call(
        scatter_kernel,
        out_shape=(
            jax.ShapeDtypeStruct((X, 1, 2, W, W), F32),
            jax.ShapeDtypeStruct((X, 1, 2, W, W), F32),
        ),
        in_specs=[SMEM, SMEM, VMEM, VMEM, VMEM] + [ANY] * 16,
        out_specs=[ANY, ANY],
        scratch_shapes=[
            pltpu.VMEM((X, 2, W, W), F32),
            pltpu.VMEM((X, 2, W, W), F32),
            pltpu.VMEM((X, 2, W, W), F32),
            pltpu.SemaphoreType.DMA((2 * X,)),
            pltpu.SemaphoreType.DMA((2 * X,)),
        ],
        name="scatter",
        cost_estimate=cost(16),
    )(strength, offsets, coupling, groups, groups.T, *early, *late, *halo_early, *halo_late)


def solution(mesh):
    placed = (
        P("energy", "section", None, None, None),
        P("section", None),
        P("section", None, None),
        P("section", None, None),
        P("section", None, None),
        P("section", None),
        P(),
        P(),
    )
    return jax.shard_map(
        per_device,
        mesh=mesh,
        in_specs=placed,
        out_specs=(
            P("energy", "section", None, None, None),
            P("energy", "section", None, None, None),
        ),
        check_vma=False,
    )
```

```python
import functools

import jax
import jax.numpy as jnp
from jax import lax
from jax.experimental import pallas as pl
from jax.experimental.pallas import tpu as pltpu
from jax.sharding import PartitionSpec as P


MODES = 3
ETA = 1.0
CONTACT = 0.6
ENERGIES = 64
W = 256
X = 4
AXES = ("energy", "section")
F32 = jnp.float32
BF16 = jnp.bfloat16

LIMIT = 24 << 20


def split(value):
    high = value.astype(BF16)
    return high, (value - high.astype(F32)).astype(BF16)


def dot(left, right):
    return lax.dot_general(left, right, (((1,), (0,)), ((), ())), preferred_element_type=F32)


def dot3(left, right):
    return dot(left[0], right[0]) + (dot(left[0], right[1]) + dot(left[1], right[0]))


def complex_split(real, imag):
    return split(real), split(imag), split(real + imag)


def complex_product(left, right):
    first = dot3(left[0], right[0])
    second = dot3(left[1], right[1])
    third = dot3(left[2], right[2])
    return first - second, third - (first + second)


def on_diagonal():
    rows = lax.broadcasted_iota(jnp.int32, (W, W), 0)
    return rows == lax.broadcasted_iota(jnp.int32, (W, W), 1)


def forward_slab(sys_re, sys_im):
    diagonal = on_diagonal()

    def inverse_diagonal(axis):
        real = jnp.sum(jnp.where(diagonal, sys_re, 0.0), axis=axis, keepdims=True)
        imag = jnp.sum(jnp.where(diagonal, sys_im, 0.0), axis=axis, keepdims=True)
        modulus = real * real + imag * imag
        return real / modulus, -imag / modulus

    col_re, col_im = inverse_diagonal(1)
    row_re, row_im = inverse_diagonal(0)
    r1_re = jnp.where(diagonal, 0.0, col_im * sys_im - col_re * sys_re)
    r1_im = jnp.where(diagonal, 0.0, -(col_re * sys_im + col_im * sys_re))
    r1 = complex_split(r1_re, r1_im)
    r2_re, r2_im = complex_product(r1, r1)
    r2 = complex_split(r2_re, r2_im)
    r3_re, r3_im = complex_product(r2, r1)
    r4_re, r4_im = complex_product(r2, r2)
    sum_re = jnp.where(diagonal, 1.0, 0.0) + r1_re + r2_re + r3_re
    sum_im = r1_im + r2_im + r3_im
    out_re, out_im = complex_product(complex_split(r4_re, r4_im), complex_split(sum_re, sum_im))
    out_re, out_im = out_re + sum_re, out_im + sum_im
    return out_re * row_re - out_im * row_im, out_re * row_im + out_im * row_re


def between_hops(left, value, right):
    return dot3(left, split(dot3(split(value), right)))


def refine(loc_re, loc_im, in_re, in_im):
    local = complex_split(loc_re, loc_im)
    half = complex_split(*complex_product(local, complex_split(in_re, in_im)))
    add_re, add_im = complex_product(half, local)
    return loc_re + add_re, loc_im + add_im


def place():
    section = lax.axis_index("section")
    return section % X, section // X, lax.axis_index("energy") % 2


def system_kernel(self_ref, onsite_ref, within_ref, first_ref, *refs):
    outs, held, hopping, sems = refs[:X], refs[X], refs[X + 1], refs[X + 2]
    x, _, _ = place()

    def order(turn):
        return (2, 1, 3, 0)[turn]

    copies = [pltpu.make_async_copy(within_ref.at[0], hopping, sems.at[X])]
    for place_at in range(X):
        turn = order(place_at)
        copies.append(
            pltpu.make_async_copy(
                self_ref.at[lax.rem(x + turn, X), 0], held.at[turn], sems.at[turn]
            )
        )
    for copy in copies:
        copy.start()
    diagonal = on_diagonal()
    copies[0].wait()
    base = 0.5 * (hopping[...] + hopping[...].T)
    hopping[...] = base + jnp.where(diagonal, onsite_ref[...], 0.0)
    for place_at in range(X):
        turn = order(place_at)
        number = first_ref[0] + lax.rem(x + turn, X)
        energy = -1.0 + (2 * number + 1).astype(F32) / ENERGIES
        copies[1 + place_at].wait()
        outs[turn][0] = jnp.where(diagonal, energy, 0.0) - hopping[...] - held[turn, 0]
        outs[turn][1] = jnp.where(diagonal, ETA, 0.0) - held[turn, 1]


def prepare_kernel(own, direct, swapped, half, other, high, low, high_t, low_t, contact, hops, sems):
    x, _, core = place()
    before, after = lax.rem(x + X - 1, X), lax.rem(x + 1, X)
    far = lax.rem(x + 2, X)
    rows = W // 2
    copies = [
        pltpu.make_async_copy(own.at[0], hops.at[x], sems.at[0]),
        pltpu.make_async_copy(direct, hops.at[jnp.where(core == 0, before, after)], sems.at[1]),
        pltpu.make_async_copy(swapped, hops.at[jnp.where(core == 0, after, before)], sems.at[2]),
        pltpu.make_async_copy(half, hops.at[far, pl.ds(core * rows, rows)], sems.at[3]),
        pltpu.make_async_copy(other, hops.at[far, pl.ds((1 - core) * rows, rows)], sems.at[4]),
    ]
    for copy in copies:
        copy.start()
    for copy in copies:
        copy.wait()
    for slab in range(X):
        high[slab], low[slab] = split(hops[slab])
        high_t[slab], low_t[slab] = split(hops[slab].T)
    contact[...] = CONTACT * dot3((high_t[0], low_t[0]), (high[0], low[0]))


def hop_of(parts, slab):
    return (parts[0][slab], parts[1][slab]), (parts[2][slab], parts[3][slab])


def advance(blocks, slab, parts, prev_re, prev_im):
    hop, hop_t = hop_of(parts, slab)
    sys_re = blocks[slab, 0] - between_hops(hop_t, prev_re, hop)
    sys_im = blocks[slab, 1] - between_hops(hop_t, prev_im, hop)
    return forward_slab(sys_re, sys_im)


def first_kernel(*refs):
    ins, moved, contact, parts, blocks, message, sems = (
        refs[:X], refs[X], refs[X + 1], refs[X + 2 : X + 6], refs[X + 6], refs[X + 7], refs[X + 8],
    )
    x, z, core = place()

    def copy(source, slab):
        return pltpu.make_async_copy(source, blocks.at[slab], sems.at[slab])

    away = (z == 1) & (core == 1)
    for turn in range(X):
        slab = lax.rem(x - turn + X, X)
        if turn == 0:

            @pl.when(away)
            def _(slab=slab):
                copy(moved, slab).start()

            @pl.when(jnp.logical_not(away))
            def _(slab=slab):
                copy(ins[0], slab).start()
        else:
            copy(ins[turn], slab).start()

    @pl.when(z == 1)
    def _():
        for slab in range(X):
            copy(ins[0], slab).wait()

    @pl.when(z == 0)
    def _():
        copy(ins[0], 0).wait()
        blocks[0, 0], blocks[0, 1] = forward_slab(blocks[0, 0], blocks[0, 1] + contact[...])

        def step(slab, unused):
            copy(ins[0], slab).wait()
            real, imag = advance(blocks, slab, parts, blocks[slab - 1, 0], blocks[slab - 1, 1])
            blocks[slab, 0], blocks[slab, 1] = real, imag
            return unused

        lax.fori_loop(1, X, step, 0)
        message[...] = blocks[X - 1]


def second_kernel(mode, *all_refs):
    blocks, message, parts = all_refs[0], all_refs[1], all_refs[2:6]
    refs = all_refs[6 if mode == "middle" else 6 + X :]
    finished = None if mode == "middle" else all_refs[6 : 6 + X]
    if mode == "middle":
        outs, answer, work, carried, sems = refs[:X], refs[X], refs[X + 1], refs[X + 2], refs[X + 3]
    else:
        outs, work, carried, sems = refs[:X], refs[X], refs[X + 1], refs[X + 2]
        far_blocks, far_parts = blocks, parts
        blocks, parts, load_sems = refs[X + 3], refs[X + 4 : X + 8], refs[X + 8]
    x, z, _ = place()

    def loads(slab, hops):
        pairs = [(far_blocks, blocks)] + list(zip(far_parts, parts)) * hops
        return [
            pltpu.make_async_copy(far.at[slab], near.at[slab], load_sems.at[slab, i])
            for i, (far, near) in enumerate(pairs)
        ]

    def put_out(slab):
        for turn in range(X):

            @pl.when(lax.rem(x + turn, X) == slab)
            def _(turn=turn):
                pltpu.make_async_copy(work.at[slab], outs[turn], sems.at[turn]).start()

    def emit(slab, target):
        hop, hop_t = hop_of(parts, slab)
        for part in range(2):
            target[part] = between_hops(hop, work[slab, part], hop_t)

    def retreat(slab, local, incoming):
        real, imag = refine(local[slab, 0], local[slab, 1], incoming[0], incoming[1])
        work[slab, 0], work[slab, 1] = real, imag
        put_out(slab)

    if mode == "last":

        @pl.when(z == 1)
        def _():
            copies = [
                pltpu.make_async_copy(finished[turn], outs[turn], sems.at[turn]) for turn in range(X)
            ]
            for copy in copies:
                copy.start()
            for copy in copies:
                copy.wait()

    @pl.when(z == (1 if mode == "middle" else 0))
    def _():
        if mode == "middle":
            real, imag = advance(blocks, 0, parts, message[0], message[1])
            work[0, 0], work[0, 1] = real, imag

            def forward(slab, unused):
                real, imag = advance(blocks, slab, parts, work[slab - 1, 0], work[slab - 1, 1])
                work[slab, 0], work[slab, 1] = real, imag
                return unused

            lax.fori_loop(1, X, forward, 0)
            put_out(X - 1)
            emit(X - 1, carried)

            def backward(index, unused):
                slab = X - 1 - index
                retreat(slab, work, carried)
                emit(slab, carried)
                return unused

            lax.fori_loop(1, X, backward, 0)
            answer[...] = carried[...]
        else:
            for slab in reversed(range(X)):
                for copy in loads(slab, slab > 0):
                    copy.start()
            carried[...] = message[...]

            def backward(index, unused):
                slab = X - 1 - index
                for copy in loads(slab, True):
                    copy.wait()
                retreat(slab, blocks, carried)
                emit(slab, carried)
                return unused

            lax.fori_loop(0, X - 1, backward, 0)
            for copy in loads(0, False):
                copy.wait()
            retreat(0, blocks, carried)
        for turn in range(X):
            pltpu.make_async_copy(work.at[turn], outs[turn], sems.at[turn]).wait()


ANY = pl.BlockSpec(memory_space=pl.ANY)
VMEM = pl.BlockSpec(memory_space=pltpu.VMEM)
SMEM = pl.BlockSpec(memory_space=pltpu.SMEM)
BLOCK = jax.ShapeDtypeStruct((2, W, W), F32)
MATRIX = jax.ShapeDtypeStruct((W, W), F32)
SLABS4 = jax.ShapeDtypeStruct((X, 2, W, W), F32)
PART = jax.ShapeDtypeStruct((X, W, W), BF16)


def cost(products):
    return pl.CostEstimate(flops=products * 6 * W**3, bytes_accessed=6 << 20, transcendentals=0)


def call(kernel, **options):
    def run(*operands):
        return pl.pallas_call(kernel, **options)(*operands)

    return run


def in_hbm(value):
    return pltpu.with_memory_space_constraint(value, pltpu.HBM)


def first(blocks, moved, contact, parts):
    return call(
        first_kernel,
        out_shape=(SLABS4, BLOCK),
        in_specs=[ANY] * (X + 1) + [VMEM] * 5,
        out_specs=[VMEM] * 2,
        scratch_shapes=[pltpu.SemaphoreType.DMA((X,))],
        name="recursion_first",
        compiler_params=pltpu.CompilerParams(vmem_limit_bytes=LIMIT),
        cost_estimate=cost(64),
    )(*blocks, moved, contact, *parts)


def second(mode, blocks, message, parts, after=()):
    count = X + (mode == "middle")
    near, loaded = VMEM, []
    if mode == "last":
        near = ANY
        blocks, parts = in_hbm(blocks), [in_hbm(part) for part in parts]
        loaded = [pltpu.VMEM((X, 2, W, W), F32)] + [pltpu.VMEM((X, W, W), BF16)] * 4
        loaded.append(pltpu.SemaphoreType.DMA((X, 5)))
    return call(
        functools.partial(second_kernel, mode),
        out_shape=(BLOCK,) * count,
        in_specs=[near, VMEM] + [near] * 4 + [ANY] * len(after),
        out_specs=[VMEM] * count,
        scratch_shapes=[
            pltpu.VMEM((X, 2, W, W), F32),
            pltpu.VMEM((2, W, W), F32),
            pltpu.SemaphoreType.DMA((X,)),
        ]
        + loaded,
        name=f"recursion_{mode}",
        compiler_params=pltpu.CompilerParams(vmem_limit_bytes=LIMIT),
        cost_estimate=cost(104 if mode == "middle" else 40),
    )(blocks, message, *parts, *after)


def scatter_kernel(*refs):
    strength_ref, offsets_ref, coupling_ref, groups_ref = refs[:4]
    blocks, halos = refs[4 : 4 + X], refs[4 + X : 4 + 2 * X]
    green_ref, self_ref = refs[4 + 2 * X : 6 + 2 * X]
    own, side, out, in_sems, out_sems = refs[6 + 2 * X :]
    x, _, _ = place()
    for turn in range(X):
        index = lax.rem(x - turn + X, X)
        pltpu.make_async_copy(blocks[turn], own.at[index], in_sems.at[index]).start()
        pltpu.make_async_copy(halos[turn], side.at[index], in_sems.at[X + index]).start()

    weights = []
    for distance in (1, 2):
        weights.append(
            sum(
                jnp.where(offsets_ref[mode] == distance, strength_ref[mode], 0.0)
                for mode in range(MODES)
            )
        )
    groups = jnp.broadcast_to(groups_ref[...], (W, W)).astype(F32)
    matrix = jnp.where(groups == groups.T, coupling_ref[0], 0.0)
    left, right = split(matrix), split(matrix.T)
    store = []
    for index in range(X):
        pltpu.make_async_copy(blocks[0], own.at[index], in_sems.at[index]).wait()
        copy = pltpu.make_async_copy(own.at[index], green_ref.at[index, 0], out_sems.at[index])
        copy.start()
        store.append(copy)
    for index in range(X):
        pltpu.make_async_copy(blocks[0], side.at[index], in_sems.at[X + index]).wait()

    def energy(index):
        return side[index + X] if index < 0 else own[index] if index < X else side[index - X]

    for index in range(X):
        near = energy(index - 1) + energy(index + 1)
        far = energy(index - 2) + energy(index + 2)
        total = weights[0] * near + weights[1] * far
        for part in range(2):
            out[index, part] = between_hops(left, total[part], right)
        copy = pltpu.make_async_copy(out.at[index], self_ref.at[index, 0], out_sems.at[X + index])
        copy.start()
        store.append(copy)
    for copy in store:
        copy.wait()


def send(value, pairs):
    return lax.ppermute(value, AXES, pairs)


def per_device(self_in, onsite, within, between, coupling, groups, offsets, strength):
    count, sections = lax.axis_size("energy"), lax.axis_size("section")
    _, _, core = place()
    chunks, lanes = range(count), range(sections)

    def device(chunk, section):
        return chunk * sections + section

    def shifted(section, turn):
        return section // X * X + (section + turn) % X

    def host(chunk, section):
        return chunk ^ 2 if section >= X and chunk % 2 else chunk

    half = lax.dynamic_slice_in_dim(between[0], core * (W // 2), W // 2, 0)
    direct = send(
        between[0],
        [(device(c, s), device(c, shifted(s, 1 if c % 2 == 0 else -1))) for c in chunks for s in lanes],
    )
    far = send(half, [(device(c, s), device(c, shifted(s, 2))) for c in chunks for s in lanes])
    partner = [(device(c, s), device(c ^ 1, s)) for c in chunks for s in lanes]
    received = (between, direct, send(direct, partner), far, send(far, partner))
    *parts, contact = call(
        prepare_kernel,
        out_shape=(PART,) * 4 + (MATRIX,),
        in_specs=[ANY] * 5,
        out_specs=[VMEM] * 5,
        scratch_shapes=[pltpu.VMEM((X, W, W), F32), pltpu.SemaphoreType.DMA((5,))],
        name="prepare",
        compiler_params=pltpu.CompilerParams(vmem_limit_bytes=LIMIT),
        cost_estimate=cost(1),
    )(*received)

    first_index = (lax.axis_index("energy") * X).reshape(1)
    systems = call(
        system_kernel,
        out_shape=(BLOCK,) * X,
        in_specs=[ANY, VMEM, ANY, SMEM],
        out_specs=[VMEM] * X,
        scratch_shapes=[
            pltpu.VMEM((X, 2, W, W), F32),
            pltpu.VMEM((W, W), F32),
            pltpu.SemaphoreType.DMA((X + 1,)),
        ],
        name="systems",
        compiler_params=pltpu.CompilerParams(vmem_limit_bytes=LIMIT),
    )(in_hbm(self_in), onsite, in_hbm(within), first_index)

    def exchange(values, back):
        result = []
        for turn in range(X):
            pairs = []
            for c in chunks:
                for s in lanes:
                    if turn or back or host(c, s) != c:
                        ends = (host(c, s), c) if back else (c, host(c, s))
                        pairs.append((device(ends[0], s), device(ends[1], shifted(s, turn))))
            result.append(send(values[turn], pairs))
        return result

    def halo(values):
        result = []
        for turn in range(X):
            pairs = []
            for c in chunks:
                for s in lanes:
                    target = c - 1 if (s - turn) % X < 2 else c + 1
                    if 0 <= target < count:
                        pairs.append((device(c, s), device(target, s)))
            result.append(send(values[turn], pairs))
        return result

    up = [(device(c, s), device(host(c, s + X), s + X)) for c in chunks for s in range(X)]
    down = [(target, source) for source, target in up]
    moved, *others = exchange(systems, False)
    lined_up, message = first((systems[0], *others), moved, contact, parts)
    message = send(message, up)
    *greens, message = second("middle", lined_up, message, parts)
    message = send(message, down)
    greens = second("last", lined_up, message, parts, greens)
    greens = exchange(greens, True)
    halos = halo(greens)

    return call(
        scatter_kernel,
        out_shape=(
            jax.ShapeDtypeStruct((X, 1, 2, W, W), F32),
            jax.ShapeDtypeStruct((X, 1, 2, W, W), F32),
        ),
        in_specs=[SMEM, SMEM, VMEM, VMEM] + [ANY] * (2 * X),
        out_specs=[ANY, ANY],
        scratch_shapes=[
            pltpu.VMEM((X, 2, W, W), F32),
            pltpu.VMEM((X, 2, W, W), F32),
            pltpu.VMEM((X, 2, W, W), F32),
            pltpu.SemaphoreType.DMA((2 * X,)),
            pltpu.SemaphoreType.DMA((2 * X,)),
        ],
        name="scatter",
        compiler_params=pltpu.CompilerParams(vmem_limit_bytes=LIMIT),
        cost_estimate=cost(16),
    )(strength, offsets, coupling, groups, *greens, *halos)


def solution(mesh):
    placed = (
        P("energy", "section", None, None, None),
        P("section", None),
        P("section", None, None),
        P("section", None, None),
        P("section", None, None),
        P("section", None),
        P(),
        P(),
    )


    def step(*arguments):
        return per_device(*arguments)

    step = jax.shard_map(
        step,
        mesh=mesh,
        in_specs=placed,
        out_specs=(
            P("energy", "section", None, None, None),
            P("energy", "section", None, None, None),
        ),
        check_vma=False,
    )
    return step
```

```python
import functools

import jax
import jax.numpy as jnp
from jax import lax
from jax.experimental import pallas as pl
from jax.experimental.pallas import tpu as pltpu
from jax.sharding import PartitionSpec as P


MODES = 3
ETA = 1.0
CONTACT = 0.6
ENERGIES = 64
W = 256
X = 4
AXES = ("energy", "section")
F32 = jnp.float32
BF16 = jnp.bfloat16

LIMIT = 24 << 20


def split(value):
    high = value.astype(BF16)
    return high, (value - high.astype(F32)).astype(BF16)


def dot(left, right):
    return lax.dot_general(left, right, (((1,), (0,)), ((), ())), preferred_element_type=F32)


def dot3(left, right):
    return dot(left[0], right[0]) + (dot(left[0], right[1]) + dot(left[1], right[0]))


def complex_split(real, imag):
    return split(real), split(imag), split(real + imag)


def complex_product(left, right):
    first = dot3(left[0], right[0])
    second = dot3(left[1], right[1])
    third = dot3(left[2], right[2])
    return first - second, third - (first + second)


def on_diagonal():
    rows = lax.broadcasted_iota(jnp.int32, (W, W), 0)
    return rows == lax.broadcasted_iota(jnp.int32, (W, W), 1)


def forward_slab(sys_re, sys_im):
    diagonal = on_diagonal()

    def inverse_diagonal(axis):
        real = jnp.sum(jnp.where(diagonal, sys_re, 0.0), axis=axis, keepdims=True)
        imag = jnp.sum(jnp.where(diagonal, sys_im, 0.0), axis=axis, keepdims=True)
        modulus = real * real + imag * imag
        return real / modulus, -imag / modulus

    col_re, col_im = inverse_diagonal(1)
    row_re, row_im = inverse_diagonal(0)
    r1_re = jnp.where(diagonal, 0.0, col_im * sys_im - col_re * sys_re)
    r1_im = jnp.where(diagonal, 0.0, -(col_re * sys_im + col_im * sys_re))
    r1 = complex_split(r1_re, r1_im)
    r2_re, r2_im = complex_product(r1, r1)
    r2 = complex_split(r2_re, r2_im)
    r3_re, r3_im = complex_product(r2, r1)
    r4_re, r4_im = complex_product(r2, r2)
    sum_re = jnp.where(diagonal, 1.0, 0.0) + r1_re + r2_re + r3_re
    sum_im = r1_im + r2_im + r3_im
    out_re, out_im = complex_product(complex_split(r4_re, r4_im), complex_split(sum_re, sum_im))
    out_re, out_im = out_re + sum_re, out_im + sum_im
    return out_re * row_re - out_im * row_im, out_re * row_im + out_im * row_re


def between_hops(left, value, right):
    return dot3(left, split(dot3(split(value), right)))


def refine(loc_re, loc_im, in_re, in_im):
    local = complex_split(loc_re, loc_im)
    half = complex_split(*complex_product(local, complex_split(in_re, in_im)))
    add_re, add_im = complex_product(half, local)
    return loc_re + add_re, loc_im + add_im


def place():
    section = lax.axis_index("section")
    return section % X, section // X, lax.axis_index("energy") % 2


def system_kernel(self_ref, onsite_ref, within_ref, first_ref, *refs):
    outs, held, hopping, sems = refs[:X], refs[X], refs[X + 1], refs[X + 2]
    x, _, _ = place()

    def order(turn):
        return (2, 1, 3, 0)[turn]

    copies = [pltpu.make_async_copy(within_ref.at[0], hopping, sems.at[X])]
    for place_at in range(X):
        turn = order(place_at)
        copies.append(
            pltpu.make_async_copy(
                self_ref.at[lax.rem(x + turn, X), 0], held.at[turn], sems.at[turn]
            )
        )
    for copy in copies:
        copy.start()
    diagonal = on_diagonal()
    copies[0].wait()
    base = 0.5 * (hopping[...] + hopping[...].T)
    hopping[...] = base + jnp.where(diagonal, onsite_ref[...], 0.0)
    for place_at in range(X):
        turn = order(place_at)
        number = first_ref[0] + lax.rem(x + turn, X)
        energy = -1.0 + (2 * number + 1).astype(F32) / ENERGIES
        copies[1 + place_at].wait()
        outs[turn][0] = jnp.where(diagonal, energy, 0.0) - hopping[...] - held[turn, 0]
        outs[turn][1] = jnp.where(diagonal, ETA, 0.0) - held[turn, 1]


def prepare_kernel(own, direct, swapped, half, other, high, low, high_t, low_t, contact, hops, sems):
    x, _, core = place()
    before, after = lax.rem(x + X - 1, X), lax.rem(x + 1, X)
    far = lax.rem(x + 2, X)
    rows = W // 2
    copies = [
        pltpu.make_async_copy(own.at[0], hops.at[x], sems.at[0]),
        pltpu.make_async_copy(direct, hops.at[jnp.where(core == 0, before, after)], sems.at[1]),
        pltpu.make_async_copy(swapped, hops.at[jnp.where(core == 0, after, before)], sems.at[2]),
        pltpu.make_async_copy(half, hops.at[far, pl.ds(core * rows, rows)], sems.at[3]),
        pltpu.make_async_copy(other, hops.at[far, pl.ds((1 - core) * rows, rows)], sems.at[4]),
    ]
    for copy in copies:
        copy.start()
    for copy in copies:
        copy.wait()
    for slab in range(X):
        high[slab], low[slab] = split(hops[slab])
        high_t[slab], low_t[slab] = split(hops[slab].T)
    contact[...] = CONTACT * dot3((high_t[0], low_t[0]), (high[0], low[0]))


def hop_of(parts, slab):
    return (parts[0][slab], parts[1][slab]), (parts[2][slab], parts[3][slab])


def advance(blocks, slab, parts, prev_re, prev_im):
    hop, hop_t = hop_of(parts, slab)
    sys_re = blocks[slab, 0] - between_hops(hop_t, prev_re, hop)
    sys_im = blocks[slab, 1] - between_hops(hop_t, prev_im, hop)
    return forward_slab(sys_re, sys_im)


def first_kernel(*refs):
    ins, moved, contact, parts, blocks, message, sems = (
        refs[:X], refs[X], refs[X + 1], refs[X + 2 : X + 6], refs[X + 6], refs[X + 7], refs[X + 8],
    )
    x, z, core = place()

    def copy(source, slab):
        return pltpu.make_async_copy(source, blocks.at[slab], sems.at[slab])

    away = (z == 1) & (core == 1)
    for turn in range(X):
        slab = lax.rem(x - turn + X, X)
        if turn == 0:

            @pl.when(away)
            def _(slab=slab):
                copy(moved, slab).start()

            @pl.when(jnp.logical_not(away))
            def _(slab=slab):
                copy(ins[0], slab).start()
        else:
            copy(ins[turn], slab).start()

    @pl.when(z == 1)
    def _():
        for slab in range(X):
            copy(ins[0], slab).wait()

    @pl.when(z == 0)
    def _():
        copy(ins[0], 0).wait()
        blocks[0, 0], blocks[0, 1] = forward_slab(blocks[0, 0], blocks[0, 1] + contact[...])

        def step(slab, unused):
            copy(ins[0], slab).wait()
            real, imag = advance(blocks, slab, parts, blocks[slab - 1, 0], blocks[slab - 1, 1])
            blocks[slab, 0], blocks[slab, 1] = real, imag
            return unused

        lax.fori_loop(1, X, step, 0)
        message[...] = blocks[X - 1]


def second_kernel(mode, *all_refs):
    blocks, message, parts = all_refs[0], all_refs[1], all_refs[2:6]
    refs = all_refs[6 if mode == "middle" else 6 + X :]
    finished = None if mode == "middle" else all_refs[6 : 6 + X]
    if mode == "middle":
        outs, answer, work, carried, sems = refs[:X], refs[X], refs[X + 1], refs[X + 2], refs[X + 3]
    else:
        outs, work, carried, sems = refs[:X], refs[X], refs[X + 1], refs[X + 2]
        far_blocks, far_parts = blocks, parts
        blocks, parts, load_sems = refs[X + 3], refs[X + 4 : X + 8], refs[X + 8]
    x, z, _ = place()

    def loads(slab, hops):
        pairs = [(far_blocks, blocks)] + list(zip(far_parts, parts)) * hops
        return [
            pltpu.make_async_copy(far.at[slab], near.at[slab], load_sems.at[slab, i])
            for i, (far, near) in enumerate(pairs)
        ]

    def put_out(slab):
        for turn in range(X):

            @pl.when(lax.rem(x + turn, X) == slab)
            def _(turn=turn):
                pltpu.make_async_copy(work.at[slab], outs[turn], sems.at[turn]).start()

    def emit(slab, target):
        hop, hop_t = hop_of(parts, slab)
        for part in range(2):
            target[part] = between_hops(hop, work[slab, part], hop_t)

    def retreat(slab, local, incoming):
        real, imag = refine(local[slab, 0], local[slab, 1], incoming[0], incoming[1])
        work[slab, 0], work[slab, 1] = real, imag
        put_out(slab)

    if mode == "last":

        @pl.when(z == 1)
        def _():
            copies = [
                pltpu.make_async_copy(finished[turn], outs[turn], sems.at[turn]) for turn in range(X)
            ]
            for copy in copies:
                copy.start()
            for copy in copies:
                copy.wait()

    @pl.when(z == (1 if mode == "middle" else 0))
    def _():
        if mode == "middle":
            real, imag = advance(blocks, 0, parts, message[0], message[1])
            work[0, 0], work[0, 1] = real, imag

            def forward(slab, unused):
                real, imag = advance(blocks, slab, parts, work[slab - 1, 0], work[slab - 1, 1])
                work[slab, 0], work[slab, 1] = real, imag
                return unused

            lax.fori_loop(1, X, forward, 0)
            put_out(X - 1)
            emit(X - 1, carried)

            def backward(index, unused):
                slab = X - 1 - index
                retreat(slab, work, carried)
                emit(slab, carried)
                return unused

            lax.fori_loop(1, X, backward, 0)
            answer[...] = carried[...]
        else:
            for slab in reversed(range(X)):
                for copy in loads(slab, slab > 0):
                    copy.start()
            carried[...] = message[...]

            def backward(index, unused):
                slab = X - 1 - index
                for copy in loads(slab, True):
                    copy.wait()
                retreat(slab, blocks, carried)
                emit(slab, carried)
                return unused

            lax.fori_loop(0, X - 1, backward, 0)
            for copy in loads(0, False):
                copy.wait()
            retreat(0, blocks, carried)
        for turn in range(X):
            pltpu.make_async_copy(work.at[turn], outs[turn], sems.at[turn]).wait()


ANY = pl.BlockSpec(memory_space=pl.ANY)
VMEM = pl.BlockSpec(memory_space=pltpu.VMEM)
SMEM = pl.BlockSpec(memory_space=pltpu.SMEM)
BLOCK = jax.ShapeDtypeStruct((2, W, W), F32)
MATRIX = jax.ShapeDtypeStruct((W, W), F32)
SLABS4 = jax.ShapeDtypeStruct((X, 2, W, W), F32)
PART = jax.ShapeDtypeStruct((X, W, W), BF16)


def cost(products):
    return pl.CostEstimate(flops=products * 6 * W**3, bytes_accessed=6 << 20, transcendentals=0)


def call(kernel, **options):
    def run(*operands):
        return pl.pallas_call(kernel, **options)(*operands)

    return run


def in_hbm(value):
    return pltpu.with_memory_space_constraint(value, pltpu.HBM)


def first(blocks, moved, contact, parts):
    return call(
        first_kernel,
        out_shape=(SLABS4, BLOCK),
        in_specs=[ANY] * (X + 1) + [VMEM] * 5,
        out_specs=[VMEM] * 2,
        scratch_shapes=[pltpu.SemaphoreType.DMA((X,))],
        name="recursion_first",
        compiler_params=pltpu.CompilerParams(vmem_limit_bytes=LIMIT),
        cost_estimate=cost(64),
    )(*blocks, moved, contact, *parts)


def second(mode, blocks, message, parts, after=()):
    count = X + (mode == "middle")
    near, loaded = VMEM, []
    if mode == "last":
        near = ANY
        blocks, parts = in_hbm(blocks), [in_hbm(part) for part in parts]
        loaded = [pltpu.VMEM((X, 2, W, W), F32)] + [pltpu.VMEM((X, W, W), BF16)] * 4
        loaded.append(pltpu.SemaphoreType.DMA((X, 5)))
    return call(
        functools.partial(second_kernel, mode),
        out_shape=(BLOCK,) * count,
        in_specs=[near, VMEM] + [near] * 4 + [ANY] * len(after),
        out_specs=[VMEM] * count,
        scratch_shapes=[
            pltpu.VMEM((X, 2, W, W), F32),
            pltpu.VMEM((2, W, W), F32),
            pltpu.SemaphoreType.DMA((X,)),
        ]
        + loaded,
        name=f"recursion_{mode}",
        compiler_params=pltpu.CompilerParams(vmem_limit_bytes=LIMIT),
        cost_estimate=cost(104 if mode == "middle" else 40),
    )(blocks, message, *parts, *after)


def scatter_kernel(*refs):
    strength_ref, offsets_ref, coupling_ref, groups_ref = refs[:4]
    blocks, halos = refs[4 : 4 + X], refs[4 + X : 4 + 2 * X]
    moved, risen = refs[4 + 2 * X], refs[4 + 2 * X : 4 + 3 * X]
    green_ref, self_ref = refs[4 + 3 * X : 6 + 3 * X]
    own, side, out, in_sems, out_sems = refs[6 + 3 * X :]
    x, z, core = place()

    def fetch(block, target, row, turn):
        index = lax.rem(x - turn + X, X)
        pltpu.make_async_copy(block, target.at[index], in_sems.at[row * X + index]).start()

    away = (z == 1) & (core == 1)

    @pl.when(away)
    def _():
        fetch(moved, own, 0, 0)

    @pl.when(jnp.logical_not(away))
    def _():
        fetch(blocks[0], own, 0, 0)

    for turn in range(1, X):
        fetch(blocks[turn], own, 0, turn)
    fetch(halos[0], side, 1, 0)
    for turn in range(1, X):
        above = (z == 1) & (core == 0) & (lax.rem(x - turn + X, X) >= 2)

        @pl.when(above)
        def _(turn=turn):
            fetch(risen[turn], side, 1, turn)

        @pl.when(jnp.logical_not(above))
        def _(turn=turn):
            fetch(halos[turn], side, 1, turn)

    weights = []
    for distance in (1, 2):
        weights.append(
            sum(
                jnp.where(offsets_ref[mode] == distance, strength_ref[mode], 0.0)
                for mode in range(MODES)
            )
        )
    groups = jnp.broadcast_to(groups_ref[...], (W, W)).astype(F32)
    matrix = jnp.where(groups == groups.T, coupling_ref[0], 0.0)
    left, right = split(matrix), split(matrix.T)
    store = []

    def arrive(index):
        pltpu.make_async_copy(blocks[0], own.at[index], in_sems.at[index]).wait()
        copy = pltpu.make_async_copy(own.at[index], green_ref.at[index, 0], out_sems.at[index])
        copy.start()
        store.append(copy)

    def arrive_aside(index):
        pltpu.make_async_copy(blocks[0], side.at[index], in_sems.at[X + index]).wait()

    def energy(index):
        return side[index + X] if index < 0 else own[index] if index < X else side[index - X]

    for index in range(X):
        arrive(index)
    for index in range(X):
        arrive_aside(index)
    for index in range(X):
        near = energy(index - 1) + energy(index + 1)
        far = energy(index - 2) + energy(index + 2)
        total = weights[0] * near + weights[1] * far
        for part in range(2):
            out[index, part] = between_hops(left, total[part], right)
        copy = pltpu.make_async_copy(out.at[index], self_ref.at[index, 0], out_sems.at[X + index])
        copy.start()
        store.append(copy)
    for copy in store:
        copy.wait()


def send(value, pairs):
    return lax.ppermute(value, AXES, pairs)


def per_device(self_in, onsite, within, between, coupling, groups, offsets, strength):
    count, sections = lax.axis_size("energy"), lax.axis_size("section")
    _, _, core = place()
    chunks, lanes = range(count), range(sections)

    def device(chunk, section):
        return chunk * sections + section

    def shifted(section, turn):
        return section // X * X + (section + turn) % X

    def host(chunk, section):
        return chunk ^ 2 if section >= X and chunk % 2 else chunk

    half = lax.dynamic_slice_in_dim(between[0], core * (W // 2), W // 2, 0)
    direct = send(
        between[0],
        [(device(c, s), device(c, shifted(s, 1 if c % 2 == 0 else -1))) for c in chunks for s in lanes],
    )
    far = send(half, [(device(c, s), device(c, shifted(s, 2))) for c in chunks for s in lanes])
    partner = [(device(c, s), device(c ^ 1, s)) for c in chunks for s in lanes]
    received = (between, direct, send(direct, partner), far, send(far, partner))
    *parts, contact = call(
        prepare_kernel,
        out_shape=(PART,) * 4 + (MATRIX,),
        in_specs=[ANY] * 5,
        out_specs=[VMEM] * 5,
        scratch_shapes=[pltpu.VMEM((X, W, W), F32), pltpu.SemaphoreType.DMA((5,))],
        name="prepare",
        compiler_params=pltpu.CompilerParams(vmem_limit_bytes=LIMIT),
        cost_estimate=cost(1),
    )(*received)

    first_index = (lax.axis_index("energy") * X).reshape(1)
    systems = call(
        system_kernel,
        out_shape=(BLOCK,) * X,
        in_specs=[ANY, VMEM, ANY, SMEM],
        out_specs=[VMEM] * X,
        scratch_shapes=[
            pltpu.VMEM((X, 2, W, W), F32),
            pltpu.VMEM((W, W), F32),
            pltpu.SemaphoreType.DMA((X + 1,)),
        ],
        name="systems",
        compiler_params=pltpu.CompilerParams(vmem_limit_bytes=LIMIT),
    )(in_hbm(self_in), onsite, in_hbm(within), first_index)

    def exchange(values, back):
        result = []
        for turn in range(X):
            pairs = []
            for c in chunks:
                for s in lanes:
                    if turn or host(c, s) != c:
                        ends = (host(c, s), c) if back else (c, host(c, s))
                        pairs.append((device(ends[0], s), device(ends[1], shifted(s, turn))))
            result.append(send(values[turn], pairs))
        return result

    def halo(value, turn):
        pairs = []
        for c in chunks:
            for s in lanes:
                target = c - 1 if (s - turn) % X < 2 else c + 1
                near = turn and s >= X and c % 2 and target > c
                if 0 <= target < count and not near:
                    pairs.append((device(c if turn else host(c, s), s), device(target, s)))
        return send(value, pairs)

    def rise(value, turn):
        pairs = []
        for c in chunks[1:-1:2]:
            for s in range(X + 2, 2 * X):
                pairs.append((device(host(c, s), s), device(c + 1, shifted(s, turn))))
        return send(value, pairs)

    up = [(device(c, s), device(host(c, s + X), s + X)) for c in chunks for s in range(X)]
    down = [(target, source) for source, target in up]
    moved, *others = exchange(systems, False)
    lined_up, message = first((systems[0], *others), moved, contact, parts)
    message = send(message, up)
    *greens, message = second("middle", lined_up, message, parts)
    message = send(message, down)
    greens = second("last", lined_up, message, parts, greens)
    own, hosted = greens[0], greens
    moved, *greens = exchange(greens, True)
    halos = [halo(own if turn == 0 else greens[turn - 1], turn) for turn in range(X)]
    risen = [rise(hosted[turn], turn) for turn in range(1, X)]

    return call(
        scatter_kernel,
        out_shape=(
            jax.ShapeDtypeStruct((X, 1, 2, W, W), F32),
            jax.ShapeDtypeStruct((X, 1, 2, W, W), F32),
        ),
        in_specs=[SMEM, SMEM, VMEM, VMEM] + [ANY] * (3 * X),
        out_specs=[ANY, ANY],
        scratch_shapes=[
            pltpu.VMEM((X, 2, W, W), F32),
            pltpu.VMEM((X, 2, W, W), F32),
            pltpu.VMEM((X, 2, W, W), F32),
            pltpu.SemaphoreType.DMA((2 * X,)),
            pltpu.SemaphoreType.DMA((2 * X,)),
        ],
        name="scatter",
        compiler_params=pltpu.CompilerParams(vmem_limit_bytes=LIMIT),
        cost_estimate=cost(16),
    )(strength, offsets, coupling, groups, own, *greens, *halos, moved, *risen)


def solution(mesh):
    placed = (
        P("energy", "section", None, None, None),
        P("section", None),
        P("section", None, None),
        P("section", None, None),
        P("section", None, None),
        P("section", None),
        P(),
        P(),
    )


    def step(*arguments):
        return per_device(*arguments)

    step = jax.shard_map(
        step,
        mesh=mesh,
        in_specs=placed,
        out_specs=(
            P("energy", "section", None, None, None),
            P("energy", "section", None, None, None),
        ),
        check_vma=False,
    )
    return step
```

```python
import functools

import jax
import jax.numpy as jnp
from jax import lax
from jax.experimental import pallas as pl
from jax.experimental.pallas import tpu as pltpu
from jax.sharding import PartitionSpec as P


MODES = 3
ETA = 1.0
CONTACT = 0.6
ENERGIES = 64
W = 256
X = 4
AXES = ("energy", "section")
F32 = jnp.float32
BF16 = jnp.bfloat16

LIMIT = 24 << 20


def split(value):
    high = value.astype(BF16)
    return high, (value - high.astype(F32)).astype(BF16)


def dot(left, right):
    return lax.dot_general(left, right, (((1,), (0,)), ((), ())), preferred_element_type=F32)


def dot3(left, right):
    return dot(left[0], right[0]) + (dot(left[0], right[1]) + dot(left[1], right[0]))


def complex_split(real, imag):
    return split(real), split(imag), split(real + imag)


def complex_product(left, right):
    first = dot3(left[0], right[0])
    second = dot3(left[1], right[1])
    third = dot3(left[2], right[2])
    return first - second, third - (first + second)


def on_diagonal():
    rows = lax.broadcasted_iota(jnp.int32, (W, W), 0)
    return rows == lax.broadcasted_iota(jnp.int32, (W, W), 1)


def forward_slab(sys_re, sys_im):
    diagonal = on_diagonal()

    def inverse_diagonal(axis):
        real = jnp.sum(jnp.where(diagonal, sys_re, 0.0), axis=axis, keepdims=True)
        imag = jnp.sum(jnp.where(diagonal, sys_im, 0.0), axis=axis, keepdims=True)
        modulus = real * real + imag * imag
        return real / modulus, -imag / modulus

    col_re, col_im = inverse_diagonal(1)
    row_re, row_im = inverse_diagonal(0)
    r1_re = jnp.where(diagonal, 0.0, col_im * sys_im - col_re * sys_re)
    r1_im = jnp.where(diagonal, 0.0, -(col_re * sys_im + col_im * sys_re))
    r1 = complex_split(r1_re, r1_im)
    r2_re, r2_im = complex_product(r1, r1)
    r2 = complex_split(r2_re, r2_im)
    r3_re, r3_im = complex_product(r2, r1)
    r4_re, r4_im = complex_product(r2, r2)
    sum_re = jnp.where(diagonal, 1.0, 0.0) + r1_re + r2_re + r3_re
    sum_im = r1_im + r2_im + r3_im
    out_re, out_im = complex_product(complex_split(r4_re, r4_im), complex_split(sum_re, sum_im))
    out_re, out_im = out_re + sum_re, out_im + sum_im
    return out_re * row_re - out_im * row_im, out_re * row_im + out_im * row_re


def between_hops(left, value, right):
    return dot3(left, split(dot3(split(value), right)))


def refine(loc_re, loc_im, in_re, in_im):
    local = complex_split(loc_re, loc_im)
    half = complex_split(*complex_product(local, complex_split(in_re, in_im)))
    add_re, add_im = complex_product(half, local)
    return loc_re + add_re, loc_im + add_im


def place():
    section = lax.axis_index("section")
    return section % X, section // X, lax.axis_index("energy") % 2


def system_kernel(self_ref, onsite_ref, within_ref, first_ref, *refs):
    outs, held, hopping, sems = refs[:X], refs[X], refs[X + 1], refs[X + 2]
    x, _, _ = place()

    def order(turn):
        return (2, 1, 3, 0)[turn]

    copies = [pltpu.make_async_copy(within_ref.at[0], hopping, sems.at[X])]
    for place_at in range(X):
        turn = order(place_at)
        copies.append(
            pltpu.make_async_copy(
                self_ref.at[lax.rem(x + turn, X), 0], held.at[turn], sems.at[turn]
            )
        )
    for copy in copies:
        copy.start()
    diagonal = on_diagonal()
    copies[0].wait()
    base = 0.5 * (hopping[...] + hopping[...].T)
    hopping[...] = base + jnp.where(diagonal, onsite_ref[...], 0.0)
    for place_at in range(X):
        turn = order(place_at)
        number = first_ref[0] + lax.rem(x + turn, X)
        energy = -1.0 + (2 * number + 1).astype(F32) / ENERGIES
        copies[1 + place_at].wait()
        outs[turn][0] = jnp.where(diagonal, energy, 0.0) - hopping[...] - held[turn, 0]
        outs[turn][1] = jnp.where(diagonal, ETA, 0.0) - held[turn, 1]


def prepare_kernel(own, direct, swapped, half, other, high, low, high_t, low_t, contact, hops, sems):
    x, _, core = place()
    before, after = lax.rem(x + X - 1, X), lax.rem(x + 1, X)
    far = lax.rem(x + 2, X)
    rows = W // 2
    copies = [
        pltpu.make_async_copy(own.at[0], hops.at[x], sems.at[0]),
        pltpu.make_async_copy(direct, hops.at[jnp.where(core == 0, before, after)], sems.at[1]),
        pltpu.make_async_copy(swapped, hops.at[jnp.where(core == 0, after, before)], sems.at[2]),
        pltpu.make_async_copy(half, hops.at[far, pl.ds(core * rows, rows)], sems.at[3]),
        pltpu.make_async_copy(other, hops.at[far, pl.ds((1 - core) * rows, rows)], sems.at[4]),
    ]
    for copy in copies:
        copy.start()
    for copy in copies:
        copy.wait()
    for slab in range(X):
        high[slab], low[slab] = split(hops[slab])
        high_t[slab], low_t[slab] = split(hops[slab].T)
    contact[...] = CONTACT * dot3((high_t[0], low_t[0]), (high[0], low[0]))


def hop_of(parts, slab):
    return (parts[0][slab], parts[1][slab]), (parts[2][slab], parts[3][slab])


def advance(blocks, slab, parts, prev_re, prev_im):
    hop, hop_t = hop_of(parts, slab)
    sys_re = blocks[slab, 0] - between_hops(hop_t, prev_re, hop)
    sys_im = blocks[slab, 1] - between_hops(hop_t, prev_im, hop)
    return forward_slab(sys_re, sys_im)


def first_kernel(*refs):
    ins, moved, contact, parts, blocks, message, sems = (
        refs[:X], refs[X], refs[X + 1], refs[X + 2 : X + 6], refs[X + 6], refs[X + 7], refs[X + 8],
    )
    x, z, core = place()

    def copy(source, slab):
        return pltpu.make_async_copy(source, blocks.at[slab], sems.at[slab])

    away = (z == 1) & (core == 1)
    for turn in range(X):
        slab = lax.rem(x - turn + X, X)
        if turn == 0:

            @pl.when(away)
            def _(slab=slab):
                copy(moved, slab).start()

            @pl.when(jnp.logical_not(away))
            def _(slab=slab):
                copy(ins[0], slab).start()
        else:
            copy(ins[turn], slab).start()

    @pl.when(z == 1)
    def _():
        for slab in range(X):
            copy(ins[0], slab).wait()

    @pl.when(z == 0)
    def _():
        copy(ins[0], 0).wait()
        blocks[0, 0], blocks[0, 1] = forward_slab(blocks[0, 0], blocks[0, 1] + contact[...])

        def step(slab, unused):
            copy(ins[0], slab).wait()
            real, imag = advance(blocks, slab, parts, blocks[slab - 1, 0], blocks[slab - 1, 1])
            blocks[slab, 0], blocks[slab, 1] = real, imag
            return unused

        lax.fori_loop(1, X, step, 0)
        message[...] = blocks[X - 1]


def second_kernel(mode, *all_refs):
    blocks, message, parts = all_refs[0], all_refs[1], all_refs[2:6]
    refs = all_refs[6 if mode == "middle" else 6 + X :]
    finished = None if mode == "middle" else all_refs[6 : 6 + X]
    if mode == "middle":
        outs, answer, work, carried, sems = refs[:X], refs[X], refs[X + 1], refs[X + 2], refs[X + 3]
    else:
        outs, work, carried, sems = refs[:X], refs[X], refs[X + 1], refs[X + 2]
        far_blocks, far_parts = blocks, parts
        blocks, parts, load_sems = refs[X + 3], refs[X + 4 : X + 8], refs[X + 8]
    x, z, _ = place()

    def loads(slab, hops):
        pairs = [(far_blocks, blocks)] + list(zip(far_parts, parts)) * hops
        return [
            pltpu.make_async_copy(far.at[slab], near.at[slab], load_sems.at[slab, i])
            for i, (far, near) in enumerate(pairs)
        ]

    def put_out(slab):
        for turn in range(X):

            @pl.when(lax.rem(x + turn, X) == slab)
            def _(turn=turn):
                pltpu.make_async_copy(work.at[slab], outs[turn], sems.at[turn]).start()

    def emit(slab, target):
        hop, hop_t = hop_of(parts, slab)
        for part in range(2):
            target[part] = between_hops(hop, work[slab, part], hop_t)

    def retreat(slab, local, incoming):
        real, imag = refine(local[slab, 0], local[slab, 1], incoming[0], incoming[1])
        work[slab, 0], work[slab, 1] = real, imag
        put_out(slab)

    if mode == "last":

        @pl.when(z == 1)
        def _():
            copies = [
                pltpu.make_async_copy(finished[turn], outs[turn], sems.at[turn]) for turn in range(X)
            ]
            for copy in copies:
                copy.start()
            for copy in copies:
                copy.wait()

    @pl.when(z == (1 if mode == "middle" else 0))
    def _():
        if mode == "middle":
            real, imag = advance(blocks, 0, parts, message[0], message[1])
            work[0, 0], work[0, 1] = real, imag

            def forward(slab, unused):
                real, imag = advance(blocks, slab, parts, work[slab - 1, 0], work[slab - 1, 1])
                work[slab, 0], work[slab, 1] = real, imag
                return unused

            lax.fori_loop(1, X, forward, 0)
            put_out(X - 1)
            emit(X - 1, carried)

            def backward(index, unused):
                slab = X - 1 - index
                retreat(slab, work, carried)
                emit(slab, carried)
                return unused

            lax.fori_loop(1, X, backward, 0)
            answer[...] = carried[...]
        else:
            for slab in reversed(range(X)):
                for copy in loads(slab, slab > 0):
                    copy.start()
            carried[...] = message[...]

            def backward(index, unused):
                slab = X - 1 - index
                for copy in loads(slab, True):
                    copy.wait()
                retreat(slab, blocks, carried)
                emit(slab, carried)
                return unused

            lax.fori_loop(0, X - 1, backward, 0)
            for copy in loads(0, False):
                copy.wait()
            retreat(0, blocks, carried)
        for turn in range(X):
            pltpu.make_async_copy(work.at[turn], outs[turn], sems.at[turn]).wait()


ANY = pl.BlockSpec(memory_space=pl.ANY)
VMEM = pl.BlockSpec(memory_space=pltpu.VMEM)
SMEM = pl.BlockSpec(memory_space=pltpu.SMEM)
BLOCK = jax.ShapeDtypeStruct((2, W, W), F32)
MATRIX = jax.ShapeDtypeStruct((W, W), F32)
SLABS4 = jax.ShapeDtypeStruct((X, 2, W, W), F32)
PART = jax.ShapeDtypeStruct((X, W, W), BF16)


def cost(products):
    return pl.CostEstimate(flops=products * 6 * W**3, bytes_accessed=6 << 20, transcendentals=0)


def call(kernel, **options):
    def run(*operands):
        return pl.pallas_call(kernel, **options)(*operands)

    return run


def in_hbm(value):
    return pltpu.with_memory_space_constraint(value, pltpu.HBM)


def first(blocks, moved, contact, parts):
    return call(
        first_kernel,
        out_shape=(SLABS4, BLOCK),
        in_specs=[ANY] * (X + 1) + [VMEM] * 5,
        out_specs=[VMEM] * 2,
        scratch_shapes=[pltpu.SemaphoreType.DMA((X,))],
        name="recursion_first",
        compiler_params=pltpu.CompilerParams(vmem_limit_bytes=LIMIT),
        cost_estimate=cost(64),
    )(*blocks, moved, contact, *parts)


def second(mode, blocks, message, parts, after=()):
    count = X + (mode == "middle")
    near, loaded = VMEM, []
    if mode == "last":
        near = ANY
        blocks, parts = in_hbm(blocks), [in_hbm(part) for part in parts]
        loaded = [pltpu.VMEM((X, 2, W, W), F32)] + [pltpu.VMEM((X, W, W), BF16)] * 4
        loaded.append(pltpu.SemaphoreType.DMA((X, 5)))
    return call(
        functools.partial(second_kernel, mode),
        out_shape=(BLOCK,) * count,
        in_specs=[near, VMEM] + [near] * 4 + [ANY] * len(after),
        out_specs=[VMEM] * count,
        scratch_shapes=[
            pltpu.VMEM((X, 2, W, W), F32),
            pltpu.VMEM((2, W, W), F32),
            pltpu.SemaphoreType.DMA((X,)),
        ]
        + loaded,
        name=f"recursion_{mode}",
        compiler_params=pltpu.CompilerParams(vmem_limit_bytes=LIMIT),
        cost_estimate=cost(104 if mode == "middle" else 40),
    )(blocks, message, *parts, *after)


def gather_kernel(*refs):
    coupling_ref, groups_ref, blocks, moved = refs[0], refs[1], refs[2 : 2 + X], refs[2 + X]
    green_ref, own = refs[3 + X], refs[4 + X]
    matrices, in_sems, out_sems = refs[5 + X : 9 + X], refs[9 + X], refs[10 + X]
    x, z, core = place()

    def fetch(block, turn):
        index = lax.rem(x - turn + X, X)
        pltpu.make_async_copy(block, own.at[index], in_sems.at[index]).start()

    away = (z == 1) & (core == 1)

    @pl.when(away)
    def _():
        fetch(moved, 0)

    @pl.when(jnp.logical_not(away))
    def _():
        fetch(blocks[0], 0)

    for turn in range(1, X):
        fetch(blocks[turn], turn)
    groups = jnp.broadcast_to(groups_ref[...], (W, W)).astype(F32)
    matrix = jnp.where(groups == groups.T, coupling_ref[0], 0.0)
    matrices[0][...], matrices[1][...] = split(matrix)
    matrices[2][...], matrices[3][...] = split(matrix.T)
    store = []
    for index in range(X):
        pltpu.make_async_copy(blocks[0], own.at[index], in_sems.at[index]).wait()
        store.append(
            pltpu.make_async_copy(own.at[index], green_ref.at[index, 0], out_sems.at[index])
        )
        store[-1].start()
    for copy in store:
        copy.wait()


def scatter_kernel(*refs):
    strength_ref, offsets_ref, own, matrices = refs[0], refs[1], refs[2], refs[3:7]
    halos = refs[7 : 7 + X]
    self_ref, side, out, in_sems, out_sems = refs[6 + 2 * X :]
    risen = (None, *refs[7 + X : 6 + 2 * X])
    x, z, core = place()

    def fetch(block, turn):
        index = lax.rem(x - turn + X, X)
        pltpu.make_async_copy(block, side.at[index], in_sems.at[index]).start()

    fetch(halos[0], 0)
    for turn in range(1, X):
        above = (z == 1) & (core == 0) & (lax.rem(x - turn + X, X) >= 2)

        @pl.when(above)
        def _(turn=turn):
            fetch(risen[turn], turn)

        @pl.when(jnp.logical_not(above))
        def _(turn=turn):
            fetch(halos[turn], turn)

    weights = []
    for distance in (1, 2):
        weights.append(
            sum(
                jnp.where(offsets_ref[mode] == distance, strength_ref[mode], 0.0)
                for mode in range(MODES)
            )
        )
    left = matrices[0][...], matrices[1][...]
    right = matrices[2][...], matrices[3][...]
    store = []
    for index in range(X):
        pltpu.make_async_copy(halos[0], side.at[index], in_sems.at[index]).wait()

    def energy(index):
        return side[index + X] if index < 0 else own[index] if index < X else side[index - X]

    for index in range(X):
        near = energy(index - 1) + energy(index + 1)
        far = energy(index - 2) + energy(index + 2)
        total = weights[0] * near + weights[1] * far
        for part in range(2):
            out[index, part] = between_hops(left, total[part], right)
        copy = pltpu.make_async_copy(out.at[index], self_ref.at[index, 0], out_sems.at[index])
        copy.start()
        store.append(copy)
    for copy in store:
        copy.wait()


def send(value, pairs):
    return lax.ppermute(value, AXES, pairs)


def per_device(self_in, onsite, within, between, coupling, groups, offsets, strength):
    count, sections = lax.axis_size("energy"), lax.axis_size("section")
    _, _, core = place()
    chunks, lanes = range(count), range(sections)

    def device(chunk, section):
        return chunk * sections + section

    def shifted(section, turn):
        return section // X * X + (section + turn) % X

    def host(chunk, section):
        return chunk ^ 2 if section >= X and chunk % 2 else chunk

    half = lax.dynamic_slice_in_dim(between[0], core * (W // 2), W // 2, 0)
    direct = send(
        between[0],
        [(device(c, s), device(c, shifted(s, 1 if c % 2 == 0 else -1))) for c in chunks for s in lanes],
    )
    far = send(half, [(device(c, s), device(c, shifted(s, 2))) for c in chunks for s in lanes])
    partner = [(device(c, s), device(c ^ 1, s)) for c in chunks for s in lanes]
    received = (between, direct, send(direct, partner), far, send(far, partner))
    *parts, contact = call(
        prepare_kernel,
        out_shape=(PART,) * 4 + (MATRIX,),
        in_specs=[ANY] * 5,
        out_specs=[VMEM] * 5,
        scratch_shapes=[pltpu.VMEM((X, W, W), F32), pltpu.SemaphoreType.DMA((5,))],
        name="prepare",
        compiler_params=pltpu.CompilerParams(vmem_limit_bytes=LIMIT),
        cost_estimate=cost(1),
    )(*received)

    first_index = (lax.axis_index("energy") * X).reshape(1)
    systems = call(
        system_kernel,
        out_shape=(BLOCK,) * X,
        in_specs=[ANY, VMEM, ANY, SMEM],
        out_specs=[VMEM] * X,
        scratch_shapes=[
            pltpu.VMEM((X, 2, W, W), F32),
            pltpu.VMEM((W, W), F32),
            pltpu.SemaphoreType.DMA((X + 1,)),
        ],
        name="systems",
        compiler_params=pltpu.CompilerParams(vmem_limit_bytes=LIMIT),
    )(in_hbm(self_in), onsite, in_hbm(within), first_index)

    def exchange(values, back):
        result = []
        for turn in range(X):
            pairs = []
            for c in chunks:
                for s in lanes:
                    if turn or host(c, s) != c:
                        ends = (host(c, s), c) if back else (c, host(c, s))
                        pairs.append((device(ends[0], s), device(ends[1], shifted(s, turn))))
            result.append(send(values[turn], pairs))
        return result

    def halo(value, turn):
        pairs = []
        for c in chunks:
            for s in lanes:
                target = c - 1 if (s - turn) % X < 2 else c + 1
                near = turn and s >= X and c % 2 and target > c
                if 0 <= target < count and not near:
                    pairs.append((device(c if turn else host(c, s), s), device(target, s)))
        return send(value, pairs)

    def rise(value, turn):
        pairs = []
        for c in chunks[1:-1:2]:
            for s in range(X + 2, 2 * X):
                pairs.append((device(host(c, s), s), device(c + 1, shifted(s, turn))))
        return send(value, pairs)

    up = [(device(c, s), device(host(c, s + X), s + X)) for c in chunks for s in range(X)]
    down = [(target, source) for source, target in up]
    moved, *others = exchange(systems, False)
    lined_up, message = first((systems[0], *others), moved, contact, parts)
    message = send(message, up)
    *greens, message = second("middle", lined_up, message, parts)
    message = send(message, down)
    greens = second("last", lined_up, message, parts, greens)
    own, hosted = greens[0], greens
    moved, *greens = exchange(greens, True)
    halos = [halo(own if turn == 0 else greens[turn - 1], turn) for turn in range(X)]
    risen = [rise(hosted[turn], turn) for turn in range(1, X)]

    green, own, *matrices = call(
        gather_kernel,
        out_shape=(jax.ShapeDtypeStruct((X, 1, 2, W, W), F32), SLABS4)
        + (jax.ShapeDtypeStruct((W, W), BF16),) * 4,
        in_specs=[VMEM, VMEM] + [ANY] * (X + 1),
        out_specs=[ANY] + [VMEM] * 5,
        scratch_shapes=[pltpu.SemaphoreType.DMA((X,)), pltpu.SemaphoreType.DMA((X,))],
        name="gather",
        compiler_params=pltpu.CompilerParams(vmem_limit_bytes=LIMIT),
        cost_estimate=cost(2),
    )(coupling, groups, own, *greens, moved)
    self_out = call(
        scatter_kernel,
        out_shape=jax.ShapeDtypeStruct((X, 1, 2, W, W), F32),
        in_specs=[SMEM, SMEM] + [VMEM] * 5 + [ANY] * (2 * X - 1),
        out_specs=ANY,
        scratch_shapes=[
            pltpu.VMEM((X, 2, W, W), F32),
            pltpu.VMEM((X, 2, W, W), F32),
            pltpu.SemaphoreType.DMA((X,)),
            pltpu.SemaphoreType.DMA((X,)),
        ],
        name="scatter",
        compiler_params=pltpu.CompilerParams(vmem_limit_bytes=LIMIT),
        cost_estimate=cost(16),
    )(strength, offsets, own, *matrices, *halos, *risen)
    return green, self_out


def solution(mesh):
    placed = (
        P("energy", "section", None, None, None),
        P("section", None),
        P("section", None, None),
        P("section", None, None),
        P("section", None, None),
        P("section", None),
        P(),
        P(),
    )


    def step(*arguments):
        return per_device(*arguments)

    step = jax.shard_map(
        step,
        mesh=mesh,
        in_specs=placed,
        out_specs=(
            P("energy", "section", None, None, None),
            P("energy", "section", None, None, None),
        ),
        check_vma=False,
    )
    return step
```
